32 devices in a mesh: section: 2 (over x), dp: 4 (over z), tensor: 4 (over y, core).
Axes of the slice: x: 2, y: 2, z: 4, core: 2. Of those that a mesh axis runs over, the one named last changes fastest.
Arguments:
- latents_in: bfloat16 [8, 256, 1024], P('dp', 'tensor'), may hold values from -6 to 6
- out_grad: bfloat16 [8, 256, 1024], P('dp', 'tensor'), may hold values from -6 to 6
- cond_table: bfloat16 [8, 1024], P(None, 'dp'), may hold values from -6 to 6
- cond_rows: int32 [8], replicated, may hold values from 0 to 7, each once
- w_qkv: bfloat16 [2, 1024, 3, 1024], P('section', 'dp', None, 'tensor'), may hold values from -0.1875 to 0.1875
- qv_bias: bfloat16 [2, 2, 1024], P('section', None, 'tensor'), may hold values from -3 to 3
- w_out: bfloat16 [2, 1024, 1024], P('section', 'dp', 'tensor'), may hold values from -1.5 to 1.5
- out_bias: bfloat16 [2, 1024], P('section', 'tensor'), may hold values from -3 to 3
- up_weight: bfloat16 [2, 1024, 4096], P('section', 'dp', 'tensor'), may hold values from -0.1875 to 0.1875
- up_projection_bias: bfloat16 [2, 4096], P('section', 'tensor'), may hold values from -3 to 3
- down_weight: bfloat16 [2, 1024, 4096], P('section', 'dp', 'tensor'), may hold values from -0.09375 to 0.09375
- down_projection_bias: bfloat16 [2, 1024], P('section', 'tensor'), may hold values from -3 to 3
- w_mod: bfloat16 [2, 1024, 6, 1024], P('section', 'dp', None, 'tensor'), may hold values from -0.1875 to 0.1875
- mod_bias: bfloat16 [2, 6, 1024], P('section', None, 'tensor'), may hold values from -3 to 3
Outputs:
- block_out: bfloat16 [2, 8, 256, 1024], P('section', 'dp', 'tensor')
- input_grad: float32 [2, 8, 256, 1024], P('section', 'dp', 'tensor')
- cond_grad: float32 [8, 1024], P(None, 'dp')
- grad_qkv: float32 [2, 1024, 3, 1024], P('section', 'dp', None, 'tensor')
- grad_qv_bias: float32 [2, 2, 1024], P('section', None, 'tensor')
- grad_out: float32 [2, 1024, 1024], P('section', 'dp', 'tensor')
- grad_out_bias: float32 [2, 1024], P('section', 'tensor')
- grad_up: float32 [2, 1024, 4096], P('section', 'dp', 'tensor')
- grad_up_bias: float32 [2, 4096], P('section', 'tensor')
- grad_down: float32 [2, 1024, 4096], P('section', 'dp', 'tensor')
- grad_down_bias: float32 [2, 1024], P('section', 'tensor')
- grad_mod: float32 [2, 1024, 6, 1024], P('section', 'dp', None, 'tensor')
- grad_mod_bias: float32 [2, 6, 1024], P('section', None, 'tensor')
The draws below stay inside these ranges and needn't reach their ends.
Inputs may be any that keep to these rules, and one draw needn't show every extreme that they name: cond_rows is a permutation: every row of the conditioning table is used by exactly one latent.
All inputs are finite; a program needn't handle non-finite values.
Results may differ from the reference program's by a relative error of at most 0.02.
Values may be sent and summed in bfloat16 or wider, within the bound.
No kernel may reach another device: no remote copies, remote signals or barrier semaphores. Data moves between devices by JAX's collectives and lax.ppermute only.
A program may use at most 128 MiB of HBM per device.

```python
import jax
import jax.numpy as jnp
from jax import lax

D = 1024
HEAD_DIM = 64
FF = 4096
SEQ = 256
LATENTS = 8
LAYERS = 2


def block_scale(key, dims, pieces, low, top_value):
    gain = 1.0
    for position, blocks in pieces:
        heights = jax.random.uniform(jax.random.fold_in(jax.random.fold_in(key, 6), position), (blocks,), jnp.float32, low / len(pieces), top_value / len(pieces))
        gain = gain * jnp.repeat(jnp.exp(heights), dims[position] // blocks).reshape((-1,) + (1,) * (len(dims) - 1 - position))
    return gain


def bell_draw(key, shape, spread, bound, pieces=(), dtype=jnp.bfloat16):
    result = jax.random.normal(key, shape, jnp.float32) * spread
    if len(pieces) > 0:
        result = block_scale(key, shape, pieces, -0.22, 0.18) * result
    return jnp.clip(result, min=-bound, max=bound).astype(dtype)


def setup_inputs(seed: int = 0) -> dict:
    arg_keys = jax.random.split(jax.random.key(seed), 15)
    return {
        "latents_in": bell_draw(arg_keys[0], (LATENTS, SEQ, D), 1.0, 6.0, ((0, 4), (1, 4))),
        "out_grad": bell_draw(arg_keys[1], (LATENTS, SEQ, D), 1.0, 6.0, ((0, 4), (1, 4))),
        "cond_table": bell_draw(arg_keys[2], (LATENTS, D), 1.0, 6.0, ((1, 4),)),
        "cond_rows": jax.random.permutation(arg_keys[3], LATENTS).astype(jnp.int32),
        "w_qkv": bell_draw(arg_keys[4], (LAYERS, D, 3, D), D ** -0.5, 0.1875, ((0, 2), (1, 4), (3, 4))),
        "qv_bias": bell_draw(arg_keys[5], (LAYERS, 2, D), 0.5, 3.0, ((0, 2), (2, 4))),
        "w_out": bell_draw(arg_keys[6], (LAYERS, D, D), (D // 64) ** -0.5, 1.5, ((0, 2), (1, 4), (2, 4))),
        "out_bias": bell_draw(arg_keys[7], (LAYERS, D), 0.5, 3.0, ((0, 2), (1, 4))),
        "up_weight": bell_draw(arg_keys[8], (LAYERS, D, FF), D ** -0.5, 0.1875, ((0, 2), (1, 4), (2, 4))),
        "up_projection_bias": bell_draw(arg_keys[9], (LAYERS, FF), 0.5, 3.0, ((0, 2), (1, 4))),
        "down_weight": bell_draw(arg_keys[10], (LAYERS, D, FF), FF ** -0.5, 0.09375, ((0, 2), (1, 4), (2, 4))),
        "down_projection_bias": bell_draw(arg_keys[11], (LAYERS, D), 0.5, 3.0, ((0, 2), (1, 4))),
        "w_mod": bell_draw(arg_keys[12], (LAYERS, D, 6, D), D ** -0.5, 0.1875, ((0, 2), (1, 4), (3, 4))),
        "mod_bias": bell_draw(arg_keys[13], (LAYERS, 6, D), 0.5, 3.0, ((0, 2), (2, 4))),
    }


@jax.custom_vjp
def low(v):
    return lax.optimization_barrier(v.astype(jnp.bfloat16)).astype(jnp.float32)

@jax.custom_vjp
def low_precision_backward(v):
    return v

def low_keep(v):
    return (low(v), None)

def low_pass(kept, grad):
    return (grad,)

def back_keep(v):
    return (v, None)

def back_low(kept, grad):
    return (low(grad),)
low.defvjp(low_keep, low_pass)
low_precision_backward.defvjp(back_keep, back_low)
epsilon = 1e-06
highest_precision = lax.Precision.HIGHEST

def normalize(values):
    centre = lax.optimization_barrier(jnp.mean(values, axis=-1, keepdims=True))
    centred = values - centre
    return centred * lax.rsqrt(lax.optimization_barrier(jnp.mean(centred * centred, axis=-1, keepdims=True)) + epsilon)

def attend(block):
    query, keys, values = block
    scores = low_precision_backward(jnp.einsum('qhd,khd->hqk', query, keys, precision=highest_precision) * HEAD_DIM ** (-0.5))
    probs = low(jax.nn.softmax(scores, axis=-1))
    return jnp.einsum('hqk,khd->qhd', probs, values, precision=highest_precision)

def block_layer(inputs, factors, w_qkv, qv_bias, w_out, out_bias, up_weight, up_projection_bias, down_weight, down_projection_bias):
    latents, length, width = inputs.shape
    heads = width // HEAD_DIM
    rows = [factors[:, index][:, None, :] for index in range(6)]
    mixed1 = low(normalize(inputs) * (1.0 + rows[1]) + rows[0])
    projected = jnp.einsum('lsi,ijo->lsjo', mixed1, w_qkv, precision=highest_precision)
    query = low(low_precision_backward(projected[:, :, 0] + qv_bias[0]))
    keys = low(low_precision_backward(projected[:, :, 1]))
    values = low(low_precision_backward(projected[:, :, 2] + qv_bias[1]))
    shape = (latents, length, heads, HEAD_DIM)
    attended = lax.map(jax.checkpoint(attend), (query.reshape(shape), keys.reshape(shape), values.reshape(shape)))
    attended = low(low_precision_backward(attended.reshape(latents, length, width)))
    attn_out = low_precision_backward(jnp.einsum('lsi,oi->lso', attended, w_out, precision=highest_precision) + out_bias)
    middle = inputs + rows[2] * attn_out
    second_mixed = low(normalize(middle) * (1.0 + rows[4]) + rows[3])
    before_block = low_precision_backward(jnp.einsum('gzo,oh->gzh', second_mixed, up_weight, precision=highest_precision) + up_projection_bias)
    active_rows = low(jax.nn.gelu(before_block, approximate=True))
    feedforward_output = low_precision_backward(jnp.einsum('kig,bg->kib', active_rows, down_weight, precision=highest_precision) + down_projection_bias)
    return middle + rows[5] * feedforward_output

def reference(latents_in, out_grad, cond_table, cond_rows, w_qkv, qv_bias, w_out, out_bias, up_weight, up_projection_bias, down_weight, down_projection_bias, w_mod, mod_bias):
    floats = [item.astype(jnp.float32) for item in (latents_in, cond_table, w_qkv, qv_bias, w_out, out_bias, up_weight, up_projection_bias, down_weight, down_projection_bias, w_mod, mod_bias)]
    probes = jnp.zeros((LAYERS - 1,) + latents_in.shape, jnp.float32)

    def forward(inputs, probe_all, table, wqkv, qvb, wout, outb, wup, upb, wdown, downb, wmod, modb):
        cond = jnp.take(table, cond_rows, axis=0)
        silu_cond = low(jax.nn.silu(cond))
        state = inputs
        outputs = []
        for index in range(LAYERS):
            factors = low_precision_backward(jnp.einsum('li,ijo->ljo', silu_cond, wmod[index], precision=highest_precision) + modb[index])
            state = block_layer(state, factors, wqkv[index], qvb[index], wout[index], outb[index], wup[index], upb[index], wdown[index], downb[index])
            if index + 1 < LAYERS:
                state = low_precision_backward(low(state))
                outputs.append(state)
                state = state + probe_all[index]
            else:
                outputs.append(state)
        return (state, jnp.stack(outputs))
    final, pullback, outputs = jax.vjp(forward, floats[0], probes, *floats[1:], has_aux=True)
    grads = pullback(out_grad.astype(jnp.float32))
    input_grad = jnp.concatenate([grads[0][None], grads[1]], axis=0)
    return (outputs.astype(jnp.bfloat16), input_grad, grads[2], grads[3], grads[4], grads[5], grads[6], grads[7], grads[8], grads[9], grads[10], grads[11], grads[12])
```

```python
import jax
import jax.numpy as jnp
from jax import lax
from jax.sharding import PartitionSpec as P

HEAD_DIM = 64
GROUP = ("section", "tensor")
epsilon = 1e-06
f32 = jnp.float32
bf16 = jnp.bfloat16


def normalize(values):
    centre = jnp.mean(values, axis=-1, keepdims=True)
    centred = values - centre
    inverse = lax.rsqrt(jnp.mean(centred * centred, axis=-1, keepdims=True) + epsilon)
    return (centred * inverse, inverse)


def normalize_back(upstream, normed, inverse):
    first = jnp.mean(upstream, axis=-1, keepdims=True)
    second = jnp.mean(upstream * normed, axis=-1, keepdims=True)
    return inverse * (upstream - first - normed * second)


def gelu_tanh(values):
    return jax.nn.gelu(values, approximate=True)


def dot(left, right):
    return jnp.dot(left, right, preferred_element_type=f32)


def dot_last(left, right):
    return lax.dot_general(left, right, (((1,), (1,)), ((), ())), preferred_element_type=f32)


def dot_first(left, right):
    return lax.dot_general(left, right, (((0,), (0,)), ((), ())), preferred_element_type=f32)


def tree_sum(parts):
    while len(parts) > 1:
        half = len(parts) // 2
        parts = [parts[i] + parts[i + half] for i in range(half)]
    return parts[0]


def flip_order(values, index):
    size = values.shape[0]
    rest = values.shape[1:]
    bit = 1
    while bit < size:
        pairs = values.reshape((size // (2 * bit), 2, bit) + rest)
        swapped = jnp.concatenate([pairs[:, 1:], pairs[:, :1]], axis=1)
        values = jnp.where((index & bit) != 0, swapped, pairs).reshape((size,) + rest)
        bit *= 2
    return values


class Group:
    def __init__(self):
        self.sections = lax.axis_size("section")
        self.tensors = lax.axis_size("tensor")
        self.far = self.sections * self.tensors // 2

    def perm(self, key, near):
        section_key = key % self.sections
        tensor_key = (key // self.sections) * 2 + near
        route = []
        for section in range(self.sections):
            for tensor in range(self.tensors):
                source = section * self.tensors + tensor
                target = (section ^ section_key) * self.tensors + (tensor ^ tensor_key)
                route.append((source, target))
        return route

    def send(self, values, key, near=0):
        return lax.ppermute(values, GROUP, self.perm(key, near))

    def gather(self, block):
        own = jnp.concatenate(
            [block] + [self.send(block, key) for key in range(1, self.far)], axis=0
        )
        return own, self.send(own, 0, 1)

    def scatter(self, own, partner):
        rows = own.shape[0] // self.far
        arrived = self.send(partner, 0, 1)
        both = (own.astype(f32) + arrived.astype(f32)).astype(bf16)
        parts = [both[:rows]] + [
            self.send(both[key * rows : (key + 1) * rows], key) for key in range(1, self.far)
        ]
        return tree_sum([part.astype(f32) for part in parts])

    def total(self, values):
        values = values + self.send(values, 0, 1)
        return tree_sum([values] + [self.send(values, key) for key in range(1, self.far)])


def swap(values):
    return lax.ppermute(values, "section", [(0, 1), (1, 0)])


def dp_send(values, key):
    return lax.ppermute(values, "dp", [(i, i ^ key) for i in range(lax.axis_size("dp"))])


def body(
    latents_in,
    out_grad,
    cond_table,
    cond_rows,
    w_qkv,
    qv_bias,
    w_out,
    out_bias,
    up_weight,
    up_projection_bias,
    down_weight,
    down_projection_bias,
    w_mod,
    mod_bias,
):
    group = Group()
    sections, tensors, far = group.sections, group.tensors, group.far
    members = sections * tensors
    layers = sections
    copies = lax.axis_size("dp")
    section = lax.axis_index("section")
    column = lax.axis_index("tensor")
    copy = lax.axis_index("dp")
    micro, local_rows, width = latents_in.shape
    rows = local_rows // sections
    block = micro * rows
    quarter = w_qkv.shape[3]
    part = quarter // sections
    hidden = up_weight.shape[2] // sections
    heads = part // HEAD_DIM
    length = rows * members
    scale = HEAD_DIM ** (-0.5)
    first = section == 0

    def halves(values):
        cut = values.reshape(values.shape[:-1] + (sections, values.shape[-1] // sections))
        keep = lax.dynamic_index_in_dim(cut, section, cut.ndim - 2, keepdims=False)
        send = lax.dynamic_index_in_dim(cut, 1 - section, cut.ndim - 2, keepdims=False)
        return keep, send

    def by_layer(keep, arrived):
        return [jnp.where(first, keep, arrived), jnp.where(first, arrived, keep)]

    def rows_of(values):
        return values.reshape(values.shape[0], -1)

    pieces = []
    qkv_keep, qkv_send = halves(w_qkv[0])
    pieces.append((rows_of(qkv_keep), rows_of(qkv_send)))
    out_keep, out_send = halves(w_out[0])
    up_keep, up_send = halves(up_weight[0])
    pieces.append(
        (
            jnp.concatenate([out_keep, up_keep], axis=1),
            jnp.concatenate([out_send, up_send], axis=1),
        )
    )
    pieces.append(halves(down_weight[0]))
    pieces = [by_layer(keep, swap(send)) for keep, send in pieces]
    full = [
        [lax.all_gather(piece[layer], "dp", axis=0, tiled=True) for piece in pieces]
        for layer in range(layers)
    ]
    weights = [
        (qkv, out_up[:, :part], out_up[:, part:], down) for qkv, out_up, down in full
    ]
    bias_local = jnp.concatenate([qv_bias[0, 0], qv_bias[0, 1]]).reshape(2, sections, part)
    bias_keep, bias_send = halves(
        jnp.concatenate(
            [
                bias_local.transpose(1, 0, 2).reshape(sections, 2 * part),
                up_projection_bias[0].reshape(sections, hidden),
            ],
            axis=1,
        ).reshape(-1)
    )
    biases = by_layer(bias_keep.astype(f32), swap(bias_send.astype(f32)))
    offset = column * quarter

    def own_row(values, layer):
        row = lax.dynamic_update_slice(
            jnp.zeros((width,), f32), values[0].astype(f32), (offset,)
        )
        return jnp.where(section == layer, row, 0.0)

    latents = cond_rows.shape[0]
    order = ((copy ^ jnp.arange(copies, dtype=jnp.int32))[:, None] * micro) + jnp.arange(
        micro, dtype=jnp.int32
    )
    mine = (order.reshape(-1)[:, None] == jnp.arange(latents, dtype=jnp.int32)[None, :])
    used_rows = jnp.sum(jnp.where(mine, cond_rows[None, :], 0), axis=1)
    picker = (used_rows[:, None] == jnp.arange(latents, dtype=jnp.int32)[None, :]).astype(bf16)
    cond_part = dot(picker, cond_table)
    silu_low = jax.nn.silu(cond_part).astype(bf16)
    mod_rows = w_mod[0].reshape(w_mod.shape[1], -1)
    mod_terms = dot(silu_low, mod_rows).reshape(copies, micro, 6, quarter)
    mod_mine = tree_sum([mod_terms[0]] + [dp_send(mod_terms[k], k) for k in range(1, copies)])
    mod_mine = mod_mine + mod_bias[0].astype(f32)
    mod_own, mod_partner = group.gather(mod_mine[None])
    mod_all = jnp.stack([mod_own, mod_partner], axis=0)
    mod_all = mod_all.reshape((2, tensors // 2, sections) + mod_mine.shape)
    mod_all = mod_all.transpose(2, 1, 0, 3, 4, 5).reshape((members,) + mod_mine.shape)
    mod_all = flip_order(mod_all, section * tensors + column)
    modulation = mod_all.reshape((sections, tensors) + mod_mine.shape)
    modulation = modulation.transpose(0, 2, 3, 1, 4).reshape(layers, micro, 6, 1, width)

    def split_latents(own, partner):
        both = jnp.stack([own, partner]).reshape(2, far, micro, rows, own.shape[-1])
        return both.transpose(2, 0, 1, 3, 4).reshape(micro, length, own.shape[-1])

    def join_latents(values):
        both = values.reshape(micro, 2, far, rows, values.shape[-1])
        both = both.transpose(1, 2, 0, 3, 4).reshape(2, far * block, values.shape[-1])
        return both[0], both[1]

    def flat(values):
        return values.reshape(block, width)

    def apart(values):
        return values.reshape(micro, rows, width)

    entry = lax.dynamic_slice_in_dim(latents_in, section * rows, rows, 1)
    kept_all = []
    out_blocks = []
    for layer in range(layers):
        qkv_w, out_w, up_w, down_w = weights[layer]
        bias = biases[layer]
        factors = [modulation[layer][:, i] for i in range(6)]
        inputs = entry.astype(f32)
        normed1, inverse1 = normalize(inputs)
        mixed1 = (normed1 * (1.0 + factors[1]) + factors[0]).astype(bf16)
        gathered1 = group.gather(flat(mixed1))
        qkv_bias = jnp.concatenate([bias[:part], jnp.zeros((part,), f32), bias[part : 2 * part]])
        projected = [(dot(rows_in, qkv_w) + qkv_bias).astype(bf16) for rows_in in gathered1]
        projected = split_latents(*projected)
        shape = (micro, length, heads, HEAD_DIM)
        query = projected[:, :, :part].reshape(shape)
        keys = projected[:, :, part : 2 * part].reshape(shape)
        values = projected[:, :, 2 * part :].reshape(shape)
        scores = jnp.einsum("lqhd,lkhd->lhqk", query, keys, preferred_element_type=f32) * scale
        raised = jnp.exp(scores - jnp.max(scores, axis=-1, keepdims=True))
        probs = raised / jnp.sum(raised, axis=-1, keepdims=True)
        attended = jnp.einsum(
            "lhqk,lkhd->lqhd", probs.astype(bf16), values, preferred_element_type=f32
        )
        attended = join_latents(attended.reshape(micro, length, part).astype(bf16))
        out_row = own_row(out_bias, layer)
        partner_term = (dot_last(attended[1], out_w) + out_row).astype(bf16)
        own_term = (dot_last(attended[0], out_w) + out_row).astype(bf16)
        attn_out = apart(group.scatter(own_term, partner_term))
        middle = inputs + factors[2] * attn_out
        normed2, inverse2 = normalize(middle)
        mixed2 = (normed2 * (1.0 + factors[4]) + factors[3]).astype(bf16)
        gathered2 = group.gather(flat(mixed2))
        up_row = bias[2 * part :]
        before = [dot(rows_in, up_w) + up_row for rows_in in gathered2]
        active = [gelu_tanh(value).astype(bf16) for value in before]
        down_row = own_row(down_projection_bias, layer)
        partner_term = (dot_last(active[1], down_w) + down_row).astype(bf16)
        own_term = (dot_last(active[0], down_w) + down_row).astype(bf16)
        mlp_out = apart(group.scatter(own_term, partner_term))
        entry = (middle + factors[5] * mlp_out).astype(bf16)
        out_blocks.append(entry)
        kept_all.append(
            (
                factors,
                normed1,
                inverse1,
                gathered1,
                query,
                keys,
                values,
                probs,
                attended,
                attn_out,
                normed2,
                inverse2,
                gathered2,
                before,
                active,
                mlp_out,
            )
        )

    def own_layer(by_layer_values, axis):
        low, high = by_layer_values
        keep = jnp.where(first, low, high)
        arrived = swap(jnp.where(first, high, low))
        return jnp.where(
            first,
            jnp.concatenate([keep, arrived], axis=axis),
            jnp.concatenate([arrived, keep], axis=axis),
        )

    block_out = own_layer(out_blocks, 1)[None]

    upstream = lax.dynamic_slice_in_dim(out_grad, section * rows, rows, 1).astype(f32)
    input_grads = [None] * layers
    factor_sums = [None] * layers
    bias_sums = [None] * layers
    weight_grads = [None] * layers

    def reduce_rows(grad):
        return lax.psum_scatter(grad.astype(bf16), "dp", scatter_dimension=0, tiled=True)

    for layer in reversed(range(layers)):
        qkv_w, out_w, up_w, down_w = weights[layer]
        (
            factors,
            normed1,
            inverse1,
            gathered1,
            query,
            keys,
            values,
            probs,
            attended,
            attn_out,
            normed2,
            inverse2,
            gathered2,
            before,
            active,
            mlp_out,
        ) = kept_all[layer]
        gate2_grad = jnp.sum(upstream * mlp_out, axis=1)
        branch2 = (upstream * factors[5]).astype(bf16)
        down_bias_grad = jnp.sum(branch2.astype(f32), axis=(0, 1))
        whole2 = group.gather(flat(branch2))
        before_grad = [
            (jax.vjp(gelu_tanh, value)[1](dot(rows_in, down_w))[0]).astype(bf16)
            for rows_in, value in zip(whole2, before)
        ]
        partner_term = dot_last(before_grad[1], up_w).astype(bf16)
        own_term = dot_last(before_grad[0], up_w).astype(bf16)
        mixed2_grad = apart(group.scatter(own_term, partner_term))
        before_cat = jnp.concatenate(before_grad, axis=0)
        up_bias_grad = jnp.sum(before_cat.astype(f32), axis=0)
        down_grad = reduce_rows(
            dot_first(jnp.concatenate(whole2, axis=0), jnp.concatenate(active, axis=0))
        )
        up_grad = reduce_rows(dot_first(jnp.concatenate(gathered2, axis=0), before_cat))
        scale2_grad = jnp.sum(mixed2_grad * normed2, axis=1)
        shift2_grad = jnp.sum(mixed2_grad, axis=1)
        middle_grad = upstream + normalize_back(
            mixed2_grad * (1.0 + factors[4]), normed2, inverse2
        )
        gate1_grad = jnp.sum(middle_grad * attn_out, axis=1)
        branch1 = (middle_grad * factors[2]).astype(bf16)
        out_bias_grad = jnp.sum(branch1.astype(f32), axis=(0, 1))
        whole1 = group.gather(flat(branch1))
        attended_grad = [dot(rows_in, out_w).astype(bf16) for rows_in in whole1]
        grad_heads = split_latents(*attended_grad).reshape(query.shape)
        value_grad = jnp.einsum(
            "lhqk,lqhd->lkhd", probs.astype(bf16), grad_heads, preferred_element_type=f32
        ).astype(bf16)
        prob_grad = jnp.einsum("lqhd,lkhd->lhqk", grad_heads, values, preferred_element_type=f32)
        score_grad = (
            probs * (prob_grad - jnp.sum(prob_grad * probs, axis=-1, keepdims=True))
        ).astype(bf16)
        query_grad = (
            jnp.einsum("lhqk,lkhd->lqhd", score_grad, keys, preferred_element_type=f32) * scale
        ).astype(bf16)
        key_grad = (
            jnp.einsum("lhqk,lqhd->lkhd", score_grad, query, preferred_element_type=f32) * scale
        ).astype(bf16)
        stacked = jnp.concatenate(
            [grad.reshape(micro, length, part) for grad in (query_grad, key_grad, value_grad)],
            axis=2,
        )
        stacked = join_latents(stacked)
        partner_term = dot_last(stacked[1], qkv_w).astype(bf16)
        own_term = dot_last(stacked[0], qkv_w).astype(bf16)
        mixed1_grad = apart(group.scatter(own_term, partner_term))
        stacked_cat = jnp.concatenate(stacked, axis=0)
        stacked_sum = jnp.sum(stacked_cat.astype(f32), axis=0)
        out_w_grad = dot_first(jnp.concatenate(whole1, axis=0), jnp.concatenate(attended, axis=0))
        qkv_grad = dot_first(jnp.concatenate(gathered1, axis=0), stacked_cat)
        attn_grad = reduce_rows(jnp.concatenate([qkv_grad, out_w_grad], axis=1))
        scale1_grad = jnp.sum(mixed1_grad * normed1, axis=1)
        shift1_grad = jnp.sum(mixed1_grad, axis=1)
        entry_grad = middle_grad + normalize_back(
            mixed1_grad * (1.0 + factors[1]), normed1, inverse1
        )
        input_grads[layer] = entry_grad.astype(bf16)
        factor_grad = jnp.stack(
            [shift1_grad, scale1_grad, gate1_grad, shift2_grad, scale2_grad, gate2_grad], axis=1
        )
        factor_sums[layer] = jnp.concatenate(
            [
                factor_grad.reshape(micro * 6, width),
                out_bias_grad[None],
                down_bias_grad[None],
            ],
            axis=0,
        )
        bias_sums[layer] = jnp.concatenate(
            [stacked_sum[:part], stacked_sum[2 * part :], up_bias_grad]
        )
        weight_grads[layer] = (attn_grad, up_grad, down_grad)
        upstream = input_grads[layer].astype(f32)

    input_grad = own_layer(input_grads, 1).astype(f32)[None]

    count = micro * 6 + 2
    pieces = jnp.stack(factor_sums).reshape(layers, count, tensors, quarter)
    pieces = pieces.transpose(0, 2, 1, 3).reshape(members, count, quarter)
    pieces = flip_order(pieces, section * tensors + column)
    pieces = pieces.reshape(sections, tensors // 2, 2, count, quarter)
    pieces = pieces.transpose(2, 1, 0, 3, 4).reshape(2, far, count, quarter)
    arrived = group.send(pieces[1], 0, 1)
    pieces = pieces[0] + arrived
    summed = tree_sum([pieces[0]] + [group.send(pieces[key], key) for key in range(1, far)])
    factor_mine = summed[: micro * 6].astype(bf16).astype(f32)
    wide = 2 * part + hidden
    bias_keep = jnp.where(first, bias_sums[0], bias_sums[1])
    bias_arrived = swap(jnp.where(first, bias_sums[1], bias_sums[0]))
    bias_mine = jnp.where(
        first,
        jnp.concatenate([bias_keep, bias_arrived]),
        jnp.concatenate([bias_arrived, bias_keep]),
    ).reshape(-1, quarter)
    small = jnp.concatenate([factor_mine, summed[micro * 6 :], bias_mine], axis=0)
    every = [small] + [dp_send(small, key) for key in range(1, copies)]
    factor_every = jnp.stack([item[: micro * 6] for item in every])
    factor_low = factor_every.astype(bf16).reshape(latents, 6 * quarter)
    bias_total = tree_sum([item[micro * 6 :] for item in every])
    latent_sum = [
        sum(item[: micro * 6].reshape(micro, 6, quarter)[i] for i in range(micro))
        for item in every
    ]
    mod_bias_grad = tree_sum(latent_sum)
    out_bias_total = bias_total[0]
    down_bias_total = bias_total[1]
    spread = bias_total[2:].reshape(sections, wide)
    q_total = spread[:, :part].reshape(quarter)
    v_total = spread[:, part : 2 * part].reshape(quarter)
    up_total = spread[:, 2 * part :].reshape(-1)
    mod_weight_grad = dot_first(silu_low, factor_low).reshape(w_mod.shape[1], 6, quarter)
    silu_grad = dot_last(factor_low, mod_rows)
    cond_part_grad = jax.vjp(jax.nn.silu, cond_part)[1](silu_grad)[0]
    table_part = jnp.dot(
        picker.astype(f32).T, cond_part_grad, precision=lax.Precision.HIGHEST
    )
    cond_grad = group.total(table_part)

    def mine_of(index, cut):
        by_layer_values = [
            grads[index].reshape(grads[index].shape[0], cut, 1, -1) for grads in weight_grads
        ]
        return own_layer(by_layer_values, 2).astype(f32)

    attn_all = mine_of(0, 4).reshape(-1, 4, quarter)
    qkv_out = attn_all[:, :3]
    out_out = attn_all[:, 3]
    up_out = mine_of(1, 1).reshape(-1, sections * hidden)
    down_out = mine_of(2, 1).reshape(-1, sections * hidden)
    return (
        block_out,
        input_grad,
        cond_grad,
        qkv_out[None],
        jnp.stack([q_total, v_total])[None],
        out_out[None],
        out_bias_total[None],
        up_out[None],
        up_total[None],
        down_out[None],
        down_bias_total[None],
        mod_weight_grad[None],
        mod_bias_grad[None],
    )


def solution(mesh):
    in_specs = (
        P("dp", "tensor", None),
        P("dp", "tensor", None),
        P(None, "dp"),
        P(),
        P("section", "dp", None, "tensor"),
        P("section", None, "tensor"),
        P("section", "dp", "tensor"),
        P("section", "tensor"),
        P("section", "dp", "tensor"),
        P("section", "tensor"),
        P("section", "dp", "tensor"),
        P("section", "tensor"),
        P("section", "dp", None, "tensor"),
        P("section", None, "tensor"),
    )
    out_specs = (
        P("section", "dp", "tensor", None),
        P("section", "dp", "tensor", None),
        P(None, "dp"),
        P("section", "dp", None, "tensor"),
        P("section", None, "tensor"),
        P("section", "dp", "tensor"),
        P("section", "tensor"),
        P("section", "dp", "tensor"),
        P("section", "tensor"),
        P("section", "dp", "tensor"),
        P("section", "tensor"),
        P("section", "dp", None, "tensor"),
        P("section", None, "tensor"),
    )
    return jax.shard_map(body, mesh=mesh, in_specs=in_specs, out_specs=out_specs, check_vma=False)
```

```python
import jax
import jax.numpy as jnp
from jax import lax
from jax.sharding import PartitionSpec as P

HEAD_DIM = 64
GROUP = ("section", "tensor")
epsilon = 1e-06
f32 = jnp.float32
bf16 = jnp.bfloat16


def normalize(values):
    centre = jnp.mean(values, axis=-1, keepdims=True)
    centred = values - centre
    inverse = lax.rsqrt(jnp.mean(centred * centred, axis=-1, keepdims=True) + epsilon)
    return (centred * inverse, inverse)


def normalize_back(upstream, normed, inverse):
    first = jnp.mean(upstream, axis=-1, keepdims=True)
    second = jnp.mean(upstream * normed, axis=-1, keepdims=True)
    return inverse * (upstream - first - normed * second)


def gelu_tanh(values):
    return jax.nn.gelu(values, approximate=True)


def dot(left, right):
    return jnp.dot(left, right, preferred_element_type=f32)


def dot_last(left, right):
    return lax.dot_general(left, right, (((1,), (1,)), ((), ())), preferred_element_type=f32)


def dot_first(left, right):
    return lax.dot_general(left, right, (((0,), (0,)), ((), ())), preferred_element_type=f32)


def tree_sum(parts):
    while len(parts) > 1:
        half = len(parts) // 2
        parts = [parts[i] + parts[i + half] for i in range(half)]
    return parts[0]


def flip_order(values, index):
    size = values.shape[0]
    rest = values.shape[1:]
    bit = 1
    while bit < size:
        pairs = values.reshape((size // (2 * bit), 2, bit) + rest)
        swapped = jnp.concatenate([pairs[:, 1:], pairs[:, :1]], axis=1)
        values = jnp.where((index & bit) != 0, swapped, pairs).reshape((size,) + rest)
        bit *= 2
    return values


class Group:
    def __init__(self):
        self.sections = lax.axis_size("section")
        self.tensors = lax.axis_size("tensor")
        self.far = self.sections * self.tensors // 2

    def perm(self, key, near):
        section_key = key % self.sections
        tensor_key = (key // self.sections) * 2 + near
        route = []
        for section in range(self.sections):
            for tensor in range(self.tensors):
                source = section * self.tensors + tensor
                target = (section ^ section_key) * self.tensors + (tensor ^ tensor_key)
                route.append((source, target))
        return route

    def send(self, values, key, near=0):
        return lax.ppermute(values, GROUP, self.perm(key, near))

    def gather(self, block):
        own = jnp.concatenate(
            [block] + [self.send(block, key) for key in range(1, self.far)], axis=0
        )
        return own, self.send(own, 0, 1)

    def scatter(self, own, partner):
        rows = own.shape[0] // self.far
        arrived = self.send(partner, 0, 1)
        both = (own.astype(f32) + arrived.astype(f32)).astype(bf16)
        parts = [both[:rows]] + [
            self.send(both[key * rows : (key + 1) * rows], key) for key in range(1, self.far)
        ]
        return tree_sum([part.astype(f32) for part in parts])

    def total(self, values):
        values = values + self.send(values, 0, 1)
        return tree_sum([values] + [self.send(values, key) for key in range(1, self.far)])


def swap(values):
    return lax.ppermute(values, "section", [(0, 1), (1, 0)])


def dp_send(values, key):
    return lax.ppermute(values, "dp", [(i, i ^ key) for i in range(lax.axis_size("dp"))])


def body(
    latents_in,
    out_grad,
    cond_table,
    cond_rows,
    w_qkv,
    qv_bias,
    w_out,
    out_bias,
    up_weight,
    up_projection_bias,
    down_weight,
    down_projection_bias,
    w_mod,
    mod_bias,
):
    group = Group()
    sections, tensors, far = group.sections, group.tensors, group.far
    members = sections * tensors
    layers = sections
    copies = lax.axis_size("dp")
    section = lax.axis_index("section")
    column = lax.axis_index("tensor")
    copy = lax.axis_index("dp")
    micro, local_rows, width = latents_in.shape
    rows = local_rows // sections
    block = micro * rows
    quarter = w_qkv.shape[3]
    part = quarter // sections
    hidden = up_weight.shape[2] // sections
    heads = part // HEAD_DIM
    length = rows * members
    scale = HEAD_DIM ** (-0.5)
    first = section == 0

    def halves(values):
        cut = values.reshape(values.shape[:-1] + (sections, values.shape[-1] // sections))
        keep = lax.dynamic_index_in_dim(cut, section, cut.ndim - 2, keepdims=False)
        send = lax.dynamic_index_in_dim(cut, 1 - section, cut.ndim - 2, keepdims=False)
        return keep, send

    def by_layer(keep, arrived):
        return [jnp.where(first, keep, arrived), jnp.where(first, arrived, keep)]

    def rows_of(values):
        return values.reshape(values.shape[0], -1)

    qkv_keep, qkv_send = halves(w_qkv[0])
    out_keep, out_send = halves(w_out[0])
    up_keep, up_send = halves(up_weight[0])
    down_keep, down_send = halves(down_weight[0])
    attn_keep = jnp.concatenate([rows_of(qkv_keep), out_keep], axis=1)
    attn_send = jnp.concatenate([rows_of(qkv_send), out_send], axis=1)
    mlp_keep = jnp.concatenate([up_keep, down_keep], axis=1)
    mlp_send = jnp.concatenate([up_send, down_send], axis=1)
    attn_arrived = swap(attn_send)
    mlp_send, cond_table, attn_arrived = lax.optimization_barrier(
        (mlp_send, cond_table, attn_arrived)
    )
    attn_pieces = by_layer(attn_keep, attn_arrived)
    mlp_pieces = by_layer(mlp_keep, swap(mlp_send))
    weights = []
    for layer in range(layers):
        attn_all = lax.all_gather(attn_pieces[layer], "dp", axis=0, tiled=True)
        mlp_all = lax.all_gather(mlp_pieces[layer], "dp", axis=0, tiled=True)
        weights.append(
            (
                attn_all[:, : 3 * part],
                attn_all[:, 3 * part :],
                mlp_all[:, :hidden],
                mlp_all[:, hidden:],
            )
        )
    bias_local = jnp.concatenate([qv_bias[0, 0], qv_bias[0, 1]]).reshape(2, sections, part)
    bias_keep, bias_send = halves(
        jnp.concatenate(
            [
                bias_local.transpose(1, 0, 2).reshape(sections, 2 * part),
                up_projection_bias[0].reshape(sections, hidden),
            ],
            axis=1,
        ).reshape(-1)
    )
    biases = by_layer(bias_keep.astype(f32), swap(bias_send.astype(f32)))
    offset = column * quarter

    def own_row(values, layer):
        row = lax.dynamic_update_slice(
            jnp.zeros((width,), f32), values[0].astype(f32), (offset,)
        )
        return jnp.where(section == layer, row, 0.0)

    latents = cond_rows.shape[0]
    order = ((copy ^ jnp.arange(copies, dtype=jnp.int32))[:, None] * micro) + jnp.arange(
        micro, dtype=jnp.int32
    )
    mine = (order.reshape(-1)[:, None] == jnp.arange(latents, dtype=jnp.int32)[None, :])
    used_rows = jnp.sum(jnp.where(mine, cond_rows[None, :], 0), axis=1)
    picker = (used_rows[:, None] == jnp.arange(latents, dtype=jnp.int32)[None, :]).astype(bf16)
    cond_part = dot(picker, cond_table)
    silu_low = jax.nn.silu(cond_part).astype(bf16)
    mod_rows = w_mod[0].reshape(w_mod.shape[1], -1)
    mod_terms = dot(silu_low, mod_rows).reshape(copies, micro, 6, quarter)
    mod_mine = tree_sum([mod_terms[0]] + [dp_send(mod_terms[k], k) for k in range(1, copies)])
    mod_mine = mod_mine + mod_bias[0].astype(f32)
    mod_own, mod_partner = group.gather(mod_mine[None])
    mod_all = jnp.stack([mod_own, mod_partner], axis=0)
    mod_all = mod_all.reshape((2, tensors // 2, sections) + mod_mine.shape)
    mod_all = mod_all.transpose(2, 1, 0, 3, 4, 5).reshape((members,) + mod_mine.shape)
    mod_all = flip_order(mod_all, section * tensors + column)
    modulation = mod_all.reshape((sections, tensors) + mod_mine.shape)
    modulation = modulation.transpose(0, 2, 3, 1, 4).reshape(layers, micro, 6, 1, width)

    def split_latents(own, partner):
        both = jnp.stack([own, partner]).reshape(2, far, micro, rows, own.shape[-1])
        return both.transpose(2, 0, 1, 3, 4).reshape(micro, length, own.shape[-1])

    def join_latents(values):
        both = values.reshape(micro, 2, far, rows, values.shape[-1])
        both = both.transpose(1, 2, 0, 3, 4).reshape(2, far * block, values.shape[-1])
        return both[0], both[1]

    def flat(values):
        return values.reshape(block, width)

    def apart(values):
        return values.reshape(micro, rows, width)

    entry = lax.dynamic_slice_in_dim(latents_in, section * rows, rows, 1)
    kept_all = []
    out_blocks = []
    for layer in range(layers):
        qkv_w, out_w, up_w, down_w = weights[layer]
        bias = biases[layer]
        factors = [modulation[layer][:, i] for i in range(6)]
        inputs = entry.astype(f32)
        normed1, inverse1 = normalize(inputs)
        mixed1 = (normed1 * (1.0 + factors[1]) + factors[0]).astype(bf16)
        gathered1 = group.gather(flat(mixed1))
        qkv_bias = jnp.concatenate([bias[:part], jnp.zeros((part,), f32), bias[part : 2 * part]])
        projected = [(dot(rows_in, qkv_w) + qkv_bias).astype(bf16) for rows_in in gathered1]
        projected = split_latents(*projected)
        shape = (micro, length, heads, HEAD_DIM)
        query = projected[:, :, :part].reshape(shape)
        keys = projected[:, :, part : 2 * part].reshape(shape)
        values = projected[:, :, 2 * part :].reshape(shape)
        scores = jnp.einsum("lqhd,lkhd->lhqk", query, keys, preferred_element_type=f32) * scale
        raised = jnp.exp(scores - jnp.max(scores, axis=-1, keepdims=True))
        probs = raised / jnp.sum(raised, axis=-1, keepdims=True)
        attended = jnp.einsum(
            "lhqk,lkhd->lqhd", probs.astype(bf16), values, preferred_element_type=f32
        )
        attended = join_latents(attended.reshape(micro, length, part).astype(bf16))
        out_row = own_row(out_bias, layer)
        partner_term = (dot_last(attended[1], out_w) + out_row).astype(bf16)
        own_term = (dot_last(attended[0], out_w) + out_row).astype(bf16)
        attn_out = apart(group.scatter(own_term, partner_term))
        middle = inputs + factors[2] * attn_out
        normed2, inverse2 = normalize(middle)
        mixed2 = (normed2 * (1.0 + factors[4]) + factors[3]).astype(bf16)
        gathered2 = group.gather(flat(mixed2))
        up_row = bias[2 * part :]
        before = [dot(rows_in, up_w) + up_row for rows_in in gathered2]
        active = [gelu_tanh(value).astype(bf16) for value in before]
        down_row = own_row(down_projection_bias, layer)
        partner_term = (dot_last(active[1], down_w) + down_row).astype(bf16)
        own_term = (dot_last(active[0], down_w) + down_row).astype(bf16)
        mlp_out = apart(group.scatter(own_term, partner_term))
        entry = (middle + factors[5] * mlp_out).astype(bf16)
        out_blocks.append(entry)
        kept_all.append(
            (
                factors,
                normed1,
                inverse1,
                gathered1,
                query,
                keys,
                values,
                probs,
                attended,
                attn_out,
                normed2,
                inverse2,
                gathered2,
                before,
                active,
                mlp_out,
            )
        )

    def own_layer(by_layer_values, axis):
        low, high = by_layer_values
        keep = jnp.where(first, low, high)
        arrived = swap(jnp.where(first, high, low))
        return jnp.where(
            first,
            jnp.concatenate([keep, arrived], axis=axis),
            jnp.concatenate([arrived, keep], axis=axis),
        )

    block_out = own_layer(out_blocks, 1)[None]

    upstream = lax.dynamic_slice_in_dim(out_grad, section * rows, rows, 1).astype(f32)
    input_grads = [None] * layers
    factor_sums = [None] * layers
    bias_sums = [None] * layers
    weight_grads = [None] * layers

    def reduce_rows(grad):
        return lax.psum_scatter(grad.astype(bf16), "dp", scatter_dimension=0, tiled=True)

    for layer in reversed(range(layers)):
        qkv_w, out_w, up_w, down_w = weights[layer]
        (
            factors,
            normed1,
            inverse1,
            gathered1,
            query,
            keys,
            values,
            probs,
            attended,
            attn_out,
            normed2,
            inverse2,
            gathered2,
            before,
            active,
            mlp_out,
        ) = kept_all[layer]
        gate2_grad = jnp.sum(upstream * mlp_out, axis=1)
        branch2 = (upstream * factors[5]).astype(bf16)
        down_bias_grad = jnp.sum(branch2.astype(f32), axis=(0, 1))
        whole2 = group.gather(flat(branch2))
        before_grad = [
            (jax.vjp(gelu_tanh, value)[1](dot(rows_in, down_w))[0]).astype(bf16)
            for rows_in, value in zip(whole2, before)
        ]
        partner_term = dot_last(before_grad[1], up_w).astype(bf16)
        own_term = dot_last(before_grad[0], up_w).astype(bf16)
        mixed2_grad = apart(group.scatter(own_term, partner_term))
        before_cat = jnp.concatenate(before_grad, axis=0)
        up_bias_grad = jnp.sum(before_cat.astype(f32), axis=0)
        down_grad = dot_first(jnp.concatenate(whole2, axis=0), jnp.concatenate(active, axis=0))
        up_grad = dot_first(jnp.concatenate(gathered2, axis=0), before_cat)
        mlp_grad = reduce_rows(jnp.concatenate([up_grad.astype(bf16), down_grad.astype(bf16)], axis=1))
        scale2_grad = jnp.sum(mixed2_grad * normed2, axis=1)
        shift2_grad = jnp.sum(mixed2_grad, axis=1)
        middle_grad = upstream + normalize_back(
            mixed2_grad * (1.0 + factors[4]), normed2, inverse2
        )
        gate1_grad = jnp.sum(middle_grad * attn_out, axis=1)
        branch1 = (middle_grad * factors[2]).astype(bf16)
        out_bias_grad = jnp.sum(branch1.astype(f32), axis=(0, 1))
        whole1 = group.gather(flat(branch1))
        attended_grad = [dot(rows_in, out_w).astype(bf16) for rows_in in whole1]
        grad_heads = split_latents(*attended_grad).reshape(query.shape)
        value_grad = jnp.einsum(
            "lhqk,lqhd->lkhd", probs.astype(bf16), grad_heads, preferred_element_type=f32
        ).astype(bf16)
        prob_grad = jnp.einsum("lqhd,lkhd->lhqk", grad_heads, values, preferred_element_type=f32)
        score_grad = (
            probs * (prob_grad - jnp.sum(prob_grad * probs, axis=-1, keepdims=True))
        ).astype(bf16)
        query_grad = (
            jnp.einsum("lhqk,lkhd->lqhd", score_grad, keys, preferred_element_type=f32) * scale
        ).astype(bf16)
        key_grad = (
            jnp.einsum("lhqk,lqhd->lkhd", score_grad, query, preferred_element_type=f32) * scale
        ).astype(bf16)
        stacked = jnp.concatenate(
            [grad.reshape(micro, length, part) for grad in (query_grad, key_grad, value_grad)],
            axis=2,
        )
        stacked = join_latents(stacked)
        partner_term = dot_last(stacked[1], qkv_w).astype(bf16)
        own_term = dot_last(stacked[0], qkv_w).astype(bf16)
        mixed1_grad = apart(group.scatter(own_term, partner_term))
        stacked_cat = jnp.concatenate(stacked, axis=0)
        stacked_sum = jnp.sum(stacked_cat.astype(f32), axis=0)
        out_w_grad = dot_first(jnp.concatenate(whole1, axis=0), jnp.concatenate(attended, axis=0))
        qkv_grad = dot_first(jnp.concatenate(gathered1, axis=0), stacked_cat)
        attn_grad = reduce_rows(jnp.concatenate([qkv_grad, out_w_grad], axis=1))
        scale1_grad = jnp.sum(mixed1_grad * normed1, axis=1)
        shift1_grad = jnp.sum(mixed1_grad, axis=1)
        entry_grad = middle_grad + normalize_back(
            mixed1_grad * (1.0 + factors[1]), normed1, inverse1
        )
        input_grads[layer] = entry_grad.astype(bf16)
        factor_grad = jnp.stack(
            [shift1_grad, scale1_grad, gate1_grad, shift2_grad, scale2_grad, gate2_grad], axis=1
        )
        factor_sums[layer] = jnp.concatenate(
            [
                factor_grad.reshape(micro * 6, width),
                out_bias_grad[None],
                down_bias_grad[None],
            ],
            axis=0,
        )
        bias_sums[layer] = jnp.concatenate(
            [stacked_sum[:part], stacked_sum[2 * part :], up_bias_grad]
        )
        weight_grads[layer] = (attn_grad, mlp_grad)
        upstream = input_grads[layer].astype(f32)

    input_grad = own_layer(input_grads, 1).astype(f32)[None]

    count = micro * 6 + 2
    pieces = jnp.stack(factor_sums).reshape(layers, count, tensors, quarter)
    pieces = pieces.transpose(0, 2, 1, 3).reshape(members, count, quarter)
    pieces = flip_order(pieces, section * tensors + column)
    pieces = pieces.reshape(sections, tensors // 2, 2, count, quarter)
    pieces = pieces.transpose(2, 1, 0, 3, 4).reshape(2, far, count, quarter)
    arrived = group.send(pieces[1], 0, 1)
    pieces = pieces[0] + arrived
    summed = tree_sum([pieces[0]] + [group.send(pieces[key], key) for key in range(1, far)])
    factor_mine = summed[: micro * 6].astype(bf16).astype(f32)
    wide = 2 * part + hidden
    bias_keep = jnp.where(first, bias_sums[0], bias_sums[1])
    bias_arrived = swap(jnp.where(first, bias_sums[1], bias_sums[0]))
    bias_mine = jnp.where(
        first,
        jnp.concatenate([bias_keep, bias_arrived]),
        jnp.concatenate([bias_arrived, bias_keep]),
    ).reshape(-1, quarter)
    small = jnp.concatenate([factor_mine, summed[micro * 6 :], bias_mine], axis=0)
    every = [small] + [dp_send(small, key) for key in range(1, copies)]
    factor_every = jnp.stack([item[: micro * 6] for item in every])
    factor_low = factor_every.astype(bf16).reshape(latents, 6 * quarter)
    bias_total = tree_sum([item[micro * 6 :] for item in every])
    latent_sum = [
        sum(item[: micro * 6].reshape(micro, 6, quarter)[i] for i in range(micro))
        for item in every
    ]
    mod_bias_grad = tree_sum(latent_sum)
    out_bias_total = bias_total[0]
    down_bias_total = bias_total[1]
    spread = bias_total[2:].reshape(sections, wide)
    q_total = spread[:, :part].reshape(quarter)
    v_total = spread[:, part : 2 * part].reshape(quarter)
    up_total = spread[:, 2 * part :].reshape(-1)
    mod_weight_grad = dot_first(silu_low, factor_low).reshape(w_mod.shape[1], 6, quarter)
    silu_grad = dot_last(factor_low, mod_rows)
    cond_part_grad = jax.vjp(jax.nn.silu, cond_part)[1](silu_grad)[0]
    table_part = jnp.dot(
        picker.astype(f32).T, cond_part_grad, precision=lax.Precision.HIGHEST
    )
    cond_grad = group.total(table_part)

    def mine_of(index, cut):
        by_layer_values = [
            grads[index].reshape(grads[index].shape[0], cut, 1, -1) for grads in weight_grads
        ]
        return own_layer(by_layer_values, 2).astype(f32)

    attn_all = mine_of(0, 4).reshape(-1, 4, quarter)
    qkv_out = attn_all[:, :3]
    out_out = attn_all[:, 3]
    mlp_all = mine_of(1, 2).reshape(-1, 2, sections * hidden)
    up_out = mlp_all[:, 0]
    down_out = mlp_all[:, 1]
    return (
        block_out,
        input_grad,
        cond_grad,
        qkv_out[None],
        jnp.stack([q_total, v_total])[None],
        out_out[None],
        out_bias_total[None],
        up_out[None],
        up_total[None],
        down_out[None],
        down_bias_total[None],
        mod_weight_grad[None],
        mod_bias_grad[None],
    )


def solution(mesh):
    in_specs = (
        P("dp", "tensor", None),
        P("dp", "tensor", None),
        P(None, "dp"),
        P(),
        P("section", "dp", None, "tensor"),
        P("section", None, "tensor"),
        P("section", "dp", "tensor"),
        P("section", "tensor"),
        P("section", "dp", "tensor"),
        P("section", "tensor"),
        P("section", "dp", "tensor"),
        P("section", "tensor"),
        P("section", "dp", None, "tensor"),
        P("section", None, "tensor"),
    )
    out_specs = (
        P("section", "dp", "tensor", None),
        P("section", "dp", "tensor", None),
        P(None, "dp"),
        P("section", "dp", None, "tensor"),
        P("section", None, "tensor"),
        P("section", "dp", "tensor"),
        P("section", "tensor"),
        P("section", "dp", "tensor"),
        P("section", "tensor"),
        P("section", "dp", "tensor"),
        P("section", "tensor"),
        P("section", "dp", None, "tensor"),
        P("section", None, "tensor"),
    )
    return jax.shard_map(body, mesh=mesh, in_specs=in_specs, out_specs=out_specs, check_vma=False)
```
